512 devices in a mesh: energy: 128 (over x_lo, z, y), space: 4 (over x_hi, core).
Axes of the slice: x: 4 (x_hi: 2, x_lo: 2; x = x_hi * 2 + x_lo), y: 8, z: 8, core: 2. Of those that a mesh axis runs over, the one named last changes fastest.
Arguments:
- greens: bfloat16 [128, 8, 3, 2, 128, 128], P('energy', 'space'), may hold values from -6 to 6
- coulomb: bfloat16 [8, 5, 128, 128], replicated, may hold values from -0.25 to 0.25
- band_mask: int32 [8, 5], replicated, may hold values 0 or 1
- window_lo: int32 [8], replicated, may hold values from 0 to 64
Outputs:
- greens_next: bfloat16 [128, 8, 3, 2, 128, 128], P('energy', 'space')
The draws below stay inside these ranges and needn't reach their ends.
All inputs are finite; a program needn't handle non-finite values.
Results may differ from the reference program's by a relative error of at most 0.0095.
Values may be sent and summed in bfloat16 or wider, within the bound.
A program may use at most 128 MiB of HBM per device.

```python
import math
import jax
import jax.numpy as jnp
from jax import lax

B = 128
BAND = 5
NE = 128
NR = 8


def set_ends(values, own_key, least, largest):
    longest = values.shape.index(max(values.shape))
    spots = []
    for shift in (0, 1):
        where = [jax.random.randint(jax.random.fold_in(own_key, axis), (), 0, length) for axis, length in enumerate(values.shape)]
        where[longest] = (where[longest] + shift) % values.shape[longest]
        spots.append(tuple(where))
    return values.at[spots[0]].set(least).at[spots[1]].set(largest)


def block_scale(key, dims, pieces, low, largest):
    loudness, own = 1.0, jax.random.fold_in(key, 6)
    for position, shards_of in pieces:
        draws = jnp.exp(jax.random.uniform(jax.random.fold_in(own, position), (shards_of,), jnp.float32, low / len(pieces), largest / len(pieces)))
        loudness = loudness * jnp.repeat(draws, dims[position] // shards_of).reshape([-1 if axis == position else 1 for axis in range(len(dims))])
    return loudness


def normal_values(rng, shape, scale, reach, shards=(), kind=jnp.bfloat16):
    gain = block_scale(rng, shape, shards, -0.22, 0.18) if shards else 1.0
    values = jax.random.normal(rng, shape, jnp.float32) * scale * gain
    return jnp.minimum(jnp.maximum(values, -reach), reach).astype(kind)


def setup_inputs(seed: int = 0) -> dict:
    seeds = jax.random.split(jax.random.key(seed), 5)
    return {
        "greens": normal_values(seeds[0], (NE, NR, 3, 2, B, B), 1.0, 6.0, ((0, 128), (1, 4))),
        "coulomb": normal_values(seeds[1], (NR, BAND, B, B), (BAND * B) ** -0.5, 0.25),
        "band_mask": set_ends((jax.random.randint(seeds[2], (NR, BAND), 0, 4) < 3).astype(jnp.int32), jax.random.fold_in(seeds[2], 1), 0, 1),
        "window_lo": set_ends(jax.random.randint(seeds[3], (NR,), 0, NE // 2 + 1), jax.random.fold_in(seeds[3], 1), 0, (NE // 2 + 1) - 1).astype(jnp.int32),
    }


def band_tile(store, shift, offset, row_count):
    if offset >= 0:
        return (store[:, 2 + shift:2 + shift + row_count, offset], False)
    start = 2 + shift + offset
    return (store[:, start:start + row_count, -offset], True)

def real_left(coulomb_tile, piece, flipped):
    right_form = 'ercjk' if flipped else 'erckj'
    return jnp.einsum('rik,' + right_form + '->ercij', coulomb_tile, piece, preferred_element_type=jnp.float32)

def complex_product(left_tile, left_flip, right_tile, right_flip):
    left_form = 'erxki' if left_flip else 'erxik'
    right_form = 'eryjk' if right_flip else 'erykj'
    products = jnp.einsum(left_form + ',' + right_form + '->erxyij', left_tile, right_tile, preferred_element_type=jnp.float32)
    return jnp.stack([products[:, :, 0, 0] - products[:, :, 1, 1], products[:, :, 0, 1] + products[:, :, 1, 0]], axis=2)

def screened_band(polar_window, coulomb_window, row_count):
    partial_rows = {}
    for extent in range(-2, 5):
        summed = None
        for middle in range(-2, 3):
            second = extent - middle
            if -2 <= second <= 2:
                coulomb_tile = coulomb_window[2:2 + row_count, middle + 2]
                piece, flipped = band_tile(polar_window, middle, second, row_count)
                term = real_left(coulomb_tile, piece, flipped)
                summed = term if summed is None else summed + term
        partial_rows[extent] = summed.astype(jnp.bfloat16)
    results = []
    for column in range(3):
        summed = None
        for extent in range(column - 2, column + 3):
            coulomb_tile = coulomb_window[2 + column:2 + column + row_count, extent - column + 2]
            term = jnp.einsum('ercik,rjk->ercij', partial_rows[extent], coulomb_tile, preferred_element_type=jnp.float32)
            summed = term if summed is None else summed + term
        results.append(summed)
    return jnp.stack(results, axis=2)

def dyson_band(green_window, sigma_window, row_count, coupling):
    left_products = {}
    for extent in range(-2, 5):
        summed = None
        for middle in range(-2, 3):
            second = extent - middle
            if -2 <= second <= 2:
                green_tile, green_flip = band_tile(green_window, 0, middle, row_count)
                sigma_tile, sigma_flip = band_tile(sigma_window, middle, second, row_count)
                term = complex_product(green_tile, green_flip, sigma_tile, sigma_flip)
                summed = term if summed is None else summed + term
        left_products[extent] = summed.astype(jnp.bfloat16)
    results = []
    for column in range(3):
        summed = None
        for extent in range(column - 2, column + 3):
            green_tile, green_flip = band_tile(green_window, extent, column - extent, row_count)
            term = complex_product(left_products[extent], False, green_tile, green_flip)
            summed = term if summed is None else summed + term
        base_tile = green_window[:, 2:2 + row_count, column].astype(jnp.float32)
        results.append(base_tile + coupling * summed)
    return jnp.stack(results, axis=2).astype(jnp.bfloat16)

def reference(greens, coulomb, band_mask, window_lo):
    energies = greens.shape[0]
    rows_all = greens.shape[1]
    width = greens.shape[-1]
    length = 2 * energies
    root = math.sqrt(energies)
    tile_rows = lax.broadcasted_iota(jnp.int32, (rows_all, 3), 0)
    tile_offsets = lax.broadcasted_iota(jnp.int32, (rows_all, 3), 1)
    kept_tiles = (tile_rows + tile_offsets < rows_all).astype(greens.dtype)
    greens = greens * kept_tiles[None, :, :, None, None, None]
    coulomb_rows = lax.broadcasted_iota(jnp.int32, (rows_all, 5), 0)
    coulomb_offsets = lax.broadcasted_iota(jnp.int32, (rows_all, 5), 1) - 2
    inside = (coulomb_rows + coulomb_offsets >= 0) & (coulomb_rows + coulomb_offsets < rows_all) & (band_mask > 0)
    masked = coulomb * inside.astype(coulomb.dtype)[:, :, None, None]
    coulomb_window = jnp.pad(masked, ((2, 2), (0, 0), (0, 0), (0, 0)))

    def correlate(row_slab):
        series = row_slab[:, :, 0].astype(jnp.float32) + 1j * row_slab[:, :, 1].astype(jnp.float32)
        spectrum = jnp.fft.fft(series, n=length, axis=0)
        mirror = jnp.roll(spectrum[::-1], 1, axis=0)
        values = jnp.fft.ifft(spectrum * mirror, axis=0)[:energies] / root
        return jnp.stack([jnp.real(values), jnp.imag(values)], axis=2).astype(jnp.bfloat16)
    polarization = jnp.moveaxis(lax.map(correlate, jnp.moveaxis(greens, 1, 0)), 0, 1)

    def screen_one(energy_slab):
        window = jnp.pad(energy_slab, ((2, 2), (0, 0), (0, 0), (0, 0), (0, 0)))[None]
        return screened_band(window, coulomb_window, rows_all)[0].astype(jnp.bfloat16)
    screened = lax.map(screen_one, polarization)

    def convolve(inputs):
        green_slab, screen_slab, lowest = inputs
        green_series = green_slab[:, :, 0].astype(jnp.float32) + 1j * green_slab[:, :, 1].astype(jnp.float32)
        screen_series = screen_slab[:, :, 0].astype(jnp.float32) + 1j * screen_slab[:, :, 1].astype(jnp.float32)
        product = jnp.fft.fft(green_series, n=length, axis=0) * jnp.fft.fft(screen_series, n=length, axis=0)
        values = jnp.fft.ifft(product, axis=0)[:energies] / root
        energy_ids = jnp.arange(energies, dtype=jnp.int32)
        active = ((energy_ids >= lowest) & (energy_ids < lowest + energies // 2)).astype(jnp.float32)
        stacked = jnp.stack([jnp.real(values), jnp.imag(values)], axis=2)
        return (stacked * active[:, None, None, None, None]).astype(jnp.bfloat16)
    self_energy = jnp.moveaxis(lax.map(convolve, (jnp.moveaxis(greens, 1, 0), jnp.moveaxis(screened, 1, 0), window_lo)), 0, 1)
    coupling = 1.0 / (5 * width)

    def update_one(inputs):
        green_slab, sigma_slab = inputs
        pads = ((2, 2), (0, 0), (0, 0), (0, 0), (0, 0))
        green_window = jnp.pad(green_slab, pads)[None]
        sigma_window = jnp.pad(sigma_slab, pads)[None]
        return dyson_band(green_window, sigma_window, rows_all, coupling)[0]
    return lax.map(update_one, (greens, self_energy))
```

```python
import functools
import math

import jax
import jax.numpy as jnp
import numpy as np
from jax import lax
from jax.experimental import pallas as pl
from jax.experimental.pallas import tpu as pltpu
from jax.sharding import PartitionSpec as P

MESH = pl.DeviceIdType.MESH
F32 = jnp.float32
BF16 = jnp.bfloat16
VMEM = pl.BlockSpec(memory_space=pltpu.VMEM)


def exchange_kernel(count, halo, src, *rest):
    if halo == "none":
        dst, send_sem, recv_sem = rest
        landed = dst
    elif halo == "src":
        dst, rims, send_sem, recv_sem, rim_send, rim_recv = rest
        landed = dst
        before, after = rims.at[0], rims.at[1]
    else:
        dst, send_sem, recv_sem, rim_send, rim_recv = rest
        landed = dst.at[1]
        before, after = dst.at[0], dst.at[2]
    me = lax.axis_index("energy")
    section = lax.axis_index("space")
    sections = lax.axis_size("space")
    following = lax.rem(section + 1, sections)
    preceding = lax.rem(section + sections - 1, sections)

    barrier = pltpu.get_barrier_semaphore()

    def greet(k, carry):
        peer = lax.rem(me + k, count)
        pl.semaphore_signal(barrier, inc=1, device_id={"energy": peer}, device_id_type=MESH)
        return carry

    lax.fori_loop(1, count, greet, 0)
    greeted = count - 1
    if halo != "none":
        for other in (following, preceding):
            pl.semaphore_signal(barrier, inc=1, device_id={"space": other}, device_id_type=MESH)
        greeted += 2
    pl.semaphore_wait(barrier, greeted)

    def rim_copies(block):
        to_following = pltpu.make_async_remote_copy(
            block, before, rim_send.at[0], rim_recv.at[0],
            device_id={"space": following}, device_id_type=MESH)
        to_preceding = pltpu.make_async_remote_copy(
            block, after, rim_send.at[1], rim_recv.at[1],
            device_id={"space": preceding}, device_id_type=MESH)
        return (to_following, to_preceding)

    def send(k, carry):
        peer = lax.rem(me + k, count)
        pltpu.make_async_remote_copy(
            src.at[peer], landed.at[me], send_sem, recv_sem,
            device_id={"energy": peer}, device_id_type=MESH).start()
        return carry

    if halo == "src":
        rims_sent = rim_copies(src)
        for copy in rims_sent:
            copy.start()
    lax.fori_loop(1, count, send, 0)
    landed[pl.ds(me, 1)] = src[pl.ds(me, 1)]
    some = pl.ds(0, count - 1)
    everything = pltpu.make_async_remote_copy(
        src.at[some], landed.at[some], send_sem, recv_sem,
        device_id={"energy": lax.rem(me + 1, count)}, device_id_type=MESH)
    everything.wait_recv()
    if halo == "dst":
        rims_sent = rim_copies(landed)
        for copy in rims_sent:
            copy.start()
    everything.wait_send()
    if halo != "none":
        for copy in rims_sent:
            copy.wait()


def exchange(blocks, halo, name):
    count = blocks.shape[0]
    slab = jax.ShapeDtypeStruct(blocks.shape, blocks.dtype)
    sems = [pltpu.SemaphoreType.DMA, pltpu.SemaphoreType.DMA]
    rim_sems = [pltpu.SemaphoreType.DMA((2,)), pltpu.SemaphoreType.DMA((2,))]
    if halo == "none":
        out_shape, scratch = slab, sems
    elif halo == "src":
        out_shape = (slab, jax.ShapeDtypeStruct((2, *blocks.shape), blocks.dtype))
        scratch = sems + rim_sems
    else:
        out_shape = jax.ShapeDtypeStruct((3, *blocks.shape), blocks.dtype)
        scratch = sems + rim_sems
    return pl.pallas_call(
        functools.partial(exchange_kernel, count, halo),
        out_shape=out_shape,
        in_specs=[VMEM],
        out_specs=jax.tree.map(lambda _: VMEM, out_shape),
        scratch_shapes=scratch,
        compiler_params=pltpu.CompilerParams(collective_id=name, has_side_effects=True),
    )(blocks)


def dot(left, right, flipped=False):
    return lax.dot_general(
        left, right, (((1,), (1 if flipped else 0,)), ((), ())), preferred_element_type=F32)


def halves(values):
    upper = values.astype(BF16)
    return upper, (values - upper.astype(F32)).astype(BF16)


def wave_tables(points):
    angle = 2.0 * math.pi * np.outer(np.arange(points) + 0.5, np.arange(points)) / (2 * points)
    cos, sin = np.cos(angle), np.sin(angle)
    forward = np.concatenate([cos, sin], axis=0)
    return halves_of(forward), halves_of(cos.T), halves_of(sin.T)


def halves_of(table):
    upper = table.astype(jnp.bfloat16)
    lower = (table - upper.astype(np.float64)).astype(jnp.bfloat16)
    return np.stack([upper, lower])


def waves(forward, re, im):
    points = re.shape[0]
    both = jnp.concatenate([re, im], axis=1)
    spectrum = dot(forward[0], both) + dot(forward[1], both)
    width = re.shape[1]
    return (spectrum[:points, :width], spectrum[points:, width:],
            spectrum[:points, width:], spectrum[points:, :width])


def unwave(table, values):
    upper, lower = halves(values)
    return dot(table[0], upper) + dot(table[0], lower) + dot(table[1], upper)


def correlate_kernel(scale, greens, forward, back_cos, out):
    for tile in range(greens.shape[0] // 2):
        a, b, c, d = waves(forward, greens[2 * tile], greens[2 * tile + 1])
        product_re = (a - b) * (a + b) - (c - d) * (c + d)
        product_im = 2.0 * (a * c + b * d)
        both = unwave(back_cos, jnp.concatenate([product_re, product_im], axis=1)) * scale
        width = a.shape[1]
        out[2 * tile] = both[:, :width].astype(BF16)
        out[2 * tile + 1] = both[:, width:].astype(BF16)


def convolve_kernel(scale, row_count, starts, greens, screened, forward, back_cos, back_sin, out):
    per_row = greens.shape[0] // (2 * row_count)
    points = greens.shape[1]
    energies = lax.broadcasted_iota(jnp.int32, (points, 2 * greens.shape[2]), 0)
    for tile in range(greens.shape[0] // 2):
        a, b, c, d = waves(forward, greens[2 * tile], greens[2 * tile + 1])
        a2, b2, c2, d2 = waves(forward, screened[2 * tile], screened[2 * tile + 1])
        even_re = (a * a2 - c * c2) + (b * b2 - d * d2)
        even_im = (a * c2 + c * a2) - (b * d2 + d * b2)
        odd_re = (a * b2 + c * d2) + (b * a2 + d * c2)
        odd_im = (c * b2 - a * d2) + (b * c2 - d * a2)
        both = unwave(back_cos, jnp.concatenate([even_re, even_im], axis=1))
        both = both + unwave(back_sin, jnp.concatenate([-odd_im, odd_re], axis=1))
        first = starts[tile // per_row]
        active = (energies >= first) & (energies < first + points // 2)
        both = jnp.where(active, both * scale, 0.0)
        width = a.shape[1]
        out[2 * tile] = both[:, :width].astype(BF16)
        out[2 * tile + 1] = both[:, width:].astype(BF16)


def screen_kernel(row_count, polar, coulomb, out, mixed):
    width = polar.shape[-1]
    for row in range(row_count):
        for extent in range(-2, 5):
            total = None
            for middle in range(-2, 3):
                second = extent - middle
                if not -2 <= second <= 2:
                    continue
                left = coulomb[2 + row, middle + 2]
                if second >= 0:
                    tile = polar[2 + row + middle, second]
                    term = dot(left, jnp.concatenate([tile[0], tile[1]], axis=1))
                else:
                    tile = polar[2 + row + extent, -second]
                    term = dot(left, jnp.concatenate([tile[0], tile[1]], axis=0), True)
                total = term if total is None else total + term
            lanes = pl.ds((extent + 2) * width, width)
            mixed[pl.ds(0, width), lanes] = total[:, :width].astype(BF16)
            mixed[pl.ds(width, width), lanes] = total[:, width:].astype(BF16)
        for column in range(3):
            right = jnp.concatenate([coulomb[2 + row + column, k] for k in range(5)], axis=1)
            result = dot(mixed[:, column * width:(column + 5) * width], right, True)
            out[row, column, 0] = result[:width].astype(BF16)
            out[row, column, 1] = result[width:].astype(BF16)


def tile_right(tile, flipped):
    re, im = tile[0], tile[1]
    if flipped:
        return jnp.concatenate(
            [jnp.concatenate([re, -im], axis=1), jnp.concatenate([im, re], axis=1)], axis=0)
    return jnp.concatenate(
        [jnp.concatenate([re, im], axis=1), jnp.concatenate([-im, re], axis=1)], axis=0)


def band(store, row, offset):
    if offset >= 0:
        return store[row, offset], False
    return store[row + offset, -offset], True


def dyson_kernel(row_count, coupling, greens, sigma, out):
    width = greens.shape[-1]
    for row in range(row_count):
        lefts = []
        for middle in range(-2, 3):
            tile, flipped = band(greens, 2 + row, middle)
            parts = [tile[0].T, tile[1].T] if flipped else [tile[0], tile[1]]
            lefts.append(jnp.concatenate(parts, axis=1))
        products = []
        for extent in range(-2, 5):
            total = None
            for middle in range(-2, 3):
                second = extent - middle
                if not -2 <= second <= 2:
                    continue
                tile, flipped = band(sigma, 2 + row + middle, second)
                term = dot(lefts[middle + 2], tile_right(tile, flipped), flipped)
                total = term if total is None else total + term
            products.append(total.astype(BF16))
        for column in range(3):
            total = None
            for extent in range(column - 2, column + 3):
                tile, flipped = band(greens, 2 + row + extent, column - extent)
                term = dot(products[extent + 2], tile_right(tile, flipped), flipped)
                total = term if total is None else total + term
            base = greens[2 + row, column]
            out[row, column, 0] = (base[0].astype(F32) + coupling * total[:, :width]).astype(BF16)
            out[row, column, 1] = (base[1].astype(F32) + coupling * total[:, width:]).astype(BF16)


def local_call(kernel, out_shape, specs, scratch=()):
    return pl.pallas_call(
        kernel, out_shape=jax.ShapeDtypeStruct(out_shape, BF16), in_specs=specs,
        out_specs=VMEM, scratch_shapes=list(scratch))


def window_of(blocks, section, sections):
    outside = jnp.stack([section > 0, section >= 0, section < sections - 1])
    blocks = jnp.where(outside[:, None, None, None, None], blocks, jnp.zeros((), blocks.dtype))
    count = blocks.shape[1]
    width = blocks.shape[-1]
    slabs = jnp.transpose(blocks.reshape(3, count, 12, width), (0, 2, 1, 3))
    return slabs.reshape(6, 3, 2, count, width)


def on_device(greens, coulomb, band_mask, window_lo):
    row_count = greens.shape[1]
    width = greens.shape[-1]
    rows_all = band_mask.shape[0]
    section = lax.axis_index("space")
    sections = lax.axis_size("space")
    energies = lax.axis_size("energy")
    first_row = section * row_count
    tile_rows = first_row + lax.broadcasted_iota(jnp.int32, (row_count, 3), 0)
    tile_offsets = lax.broadcasted_iota(jnp.int32, (row_count, 3), 1)
    kept_tiles = (tile_rows + tile_offsets < rows_all)[:, :, None, None, None]
    greens = jnp.where(kept_tiles, greens[0], jnp.zeros((), greens.dtype))

    coulomb_rows = lax.broadcasted_iota(jnp.int32, (rows_all, 5), 0)
    coulomb_offsets = lax.broadcasted_iota(jnp.int32, (rows_all, 5), 1) - 2
    inside = (
        (coulomb_rows + coulomb_offsets >= 0)
        & (coulomb_rows + coulomb_offsets < rows_all)
        & (band_mask > 0)
    )
    masked = jnp.where(inside[:, :, None, None], coulomb, jnp.zeros((), coulomb.dtype))
    padded = jnp.pad(masked, ((2, 2), (0, 0), (0, 0), (0, 0)))
    coulomb_window = lax.dynamic_slice_in_dim(padded, first_row, row_count + 4, 0)
    starts = lax.dynamic_slice_in_dim(window_lo, first_row, row_count, 0)

    slabs = row_count * 3 * 2
    message = (width, slabs // 4, 4, width)
    forward, back_cos, back_sin = wave_tables(energies)
    scale = 1.0 / (energies * math.sqrt(energies))

    def packed(tiles):
        return jnp.transpose(tiles.reshape(slabs, tiles.shape[-2], width), (1, 0, 2)).reshape(message)

    def by_slab(blocks):
        return jnp.transpose(blocks.reshape(energies, slabs, width), (1, 0, 2))

    element_shape = (slabs, energies, width)
    own = packed(greens)
    arrived, rims = exchange(own, "src", 0)
    elements = by_slab(arrived)
    polar = local_call(
        functools.partial(correlate_kernel, scale), element_shape, [VMEM] * 3,
    )(elements, forward, back_cos)
    polar_window = window_of(exchange(packed(polar), "dst", 1), section, sections)
    screened = local_call(
        functools.partial(screen_kernel, row_count), (row_count, 3, 2, width, width), [VMEM] * 2,
        [pltpu.VMEM((2 * width, 7 * width), BF16)],
    )(polar_window, coulomb_window)
    screen_elements = by_slab(exchange(packed(screened), "none", 2))
    sigma = local_call(
        functools.partial(convolve_kernel, scale, row_count), element_shape,
        [pl.BlockSpec(memory_space=pltpu.SMEM)] + [VMEM] * 5,
    )(starts, elements, screen_elements, forward, back_cos, back_sin)
    sigma_window = window_of(exchange(packed(sigma), "dst", 3), section, sections)
    green_window = window_of(jnp.stack([rims[0], own, rims[1]]), section, sections)
    updated = local_call(
        functools.partial(dyson_kernel, row_count, 1.0 / (5 * width)),
        (row_count, 3, 2, width, width), [VMEM] * 2,
    )(green_window, sigma_window)
    return updated[None]


def solution(mesh):
    return jax.shard_map(
        on_device,
        mesh=mesh,
        in_specs=(P("energy", "space", None, None, None, None), P(), P(), P()),
        out_specs=P("energy", "space", None, None, None, None),
        check_vma=False,
    )
```

```python
import functools
import math

import jax
import jax.numpy as jnp
import numpy as np
from jax import lax
from jax.experimental import pallas as pl
from jax.experimental.pallas import tpu as pltpu
from jax.sharding import PartitionSpec as P

MESH = pl.DeviceIdType.MESH
F32 = jnp.float32
BF16 = jnp.bfloat16
VMEM = pl.BlockSpec(memory_space=pltpu.VMEM)


def dot(left, right, flipped=False):
    return lax.dot_general(
        left, right, (((1,), (1 if flipped else 0,)), ((), ())), preferred_element_type=F32)


def halves(values):
    upper = values.astype(BF16)
    return upper, (values - upper.astype(F32)).astype(BF16)


def wave_tables(points):
    angle = 2.0 * math.pi * np.outer(np.arange(points) + 0.5, np.arange(points)) / (2 * points)
    cos, sin = np.cos(angle), np.sin(angle)
    forward = np.concatenate([cos, sin], axis=0)
    return halves_of(forward), halves_of(cos.T), halves_of(sin.T)


def halves_of(table):
    upper = table.astype(jnp.bfloat16)
    lower = (table - upper.astype(np.float64)).astype(jnp.bfloat16)
    return np.stack([upper, lower])


def waves(forward, re, im):
    points = re.shape[0]
    both = jnp.concatenate([re, im], axis=1)
    spectrum = dot(forward[0], both) + dot(forward[1], both)
    width = re.shape[1]
    return (spectrum[:points, :width], spectrum[points:, width:],
            spectrum[:points, width:], spectrum[points:, :width])


def unwave(table, values):
    upper, lower = halves(values)
    return dot(table[0], upper) + dot(table[0], lower) + dot(table[1], upper)


def tile_right(tile, flipped):
    re, im = tile[0], tile[1]
    if flipped:
        return jnp.concatenate(
            [jnp.concatenate([re, -im], axis=1), jnp.concatenate([im, re], axis=1)], axis=0)
    return jnp.concatenate(
        [jnp.concatenate([re, im], axis=1), jnp.concatenate([-im, re], axis=1)], axis=0)


def steps(count, body):
    lax.fori_loop(0, count, lambda k, carry: (body(k), carry)[1], 0)


def pack(tiles, blocks):
    def group(g):
        blocks[:, g] = jnp.transpose(tiles[pl.ds(4 * g, 4)], (1, 0, 2))
    steps(blocks.shape[1], group)


def unpack(blocks, tiles):
    def group(g):
        tiles[pl.ds(4 * g, 4)] = jnp.transpose(blocks[:, g], (1, 0, 2))
    steps(blocks.shape[1], group)


def far_first(k):
    return 4 + jnp.where(k % 2 == 1, -((k + 1) // 2), k // 2)


def offsets(k):
    return 1 - k // 64, far_first(k // 8 % 8), far_first(k % 8)


def update_kernel(
    coupling, greens, coulomb, mask, window_lo, forward, back_cos, back_sin, out,
    own, arrived, green_rims, polar_sent, polar_blocks, screen_sent, screen_blocks,
    sigma_sent, sigma_blocks, slabs, spectra, green_tiles, window, potential, mixed,
    send_sem, recv_sem, rim_send, rim_recv,
):
    count = lax.axis_size("energy")
    sections = lax.axis_size("space")
    me = lax.axis_index("energy")
    section = lax.axis_index("space")
    row_count, width = greens.shape[0] // 6, greens.shape[-1]
    rows_all = coulomb.shape[0]
    points = count
    first_row = section * row_count
    scale = 1.0 / (count * math.sqrt(count))
    my_x, my_z, my_y = me // 64, me // 8 % 8, me % 8
    has_before, has_after = section > 0, section < sections - 1
    some = pl.ds(0, count - 1)

    def partner(k):
        dx, dz, dy = offsets(k)
        return (my_x + dx) % 2 * 64 + (my_z + dz) % 8 * 8 + (my_y + dy) % 8

    def send_all(phase, source, landed):
        def send(k):
            peer = partner(k)
            pltpu.make_async_remote_copy(
                source.at[peer], landed.at[me], send_sem.at[phase], recv_sem.at[phase],
                device_id={"energy": peer}, device_id_type=MESH).start()
        steps(count - 1, send)
        landed[pl.ds(me, 1)] = source[pl.ds(me, 1)]

    def everything(phase, source, landed):
        return pltpu.make_async_remote_copy(
            source.at[some], landed.at[some], send_sem.at[phase], recv_sem.at[phase],
            device_id={"energy": (me + 1) % count}, device_id_type=MESH)

    def rims(phase, block, before, after):
        to_following = pltpu.make_async_remote_copy(
            block, before, rim_send.at[phase, 0], rim_recv.at[phase, 0],
            device_id={"space": (section + 1) % sections}, device_id_type=MESH)
        to_preceding = pltpu.make_async_remote_copy(
            block, after, rim_send.at[phase, 1], rim_recv.at[phase, 1],
            device_id={"space": (section + sections - 1) % sections}, device_id_type=MESH)
        return to_following, to_preceding

    def start_rims(pair):
        @pl.when(has_after)
        def _():
            pair[0].start()

        @pl.when(has_before)
        def _():
            pair[1].start()

    def end_rims(pair, before, after, tiles, rows):
        @pl.when(has_before)
        def _():
            pair[0].wait_recv()
            unpack(before, tiles.at[pl.ds(0, rows)])

        @pl.when(section == 0)
        def _():
            tiles[pl.ds(0, rows)] = jnp.zeros((rows, width, width), BF16)

        @pl.when(has_after)
        def _():
            pair[1].wait_recv()
            unpack(after, tiles.at[pl.ds(2 * rows, rows)])

        @pl.when(section == sections - 1)
        def _():
            tiles[pl.ds(2 * rows, rows)] = jnp.zeros((rows, width, width), BF16)

    def sent_rims(pair):
        @pl.when(has_after)
        def _():
            pair[0].wait_send()

        @pl.when(has_before)
        def _():
            pair[1].wait_send()

    barrier = pltpu.get_barrier_semaphore()
    steps(count - 1, lambda k: pl.semaphore_signal(
        barrier, inc=1, device_id={"energy": partner(k)}, device_id_type=MESH))
    for step in (1, sections - 1):
        pl.semaphore_signal(
            barrier, inc=1, device_id={"space": (section + step) % sections}, device_id_type=MESH)

    rows = 6 * row_count

    def keep(k):
        row, offset = k // 6, k % 6 // 2
        kept = (jnp.zeros((width, width), jnp.int32) + (first_row + row + offset)) < rows_all
        green_tiles[rows + k] = jnp.where(kept, greens[k], jnp.zeros((), BF16))
    steps(rows, keep)
    pack(green_tiles.at[pl.ds(rows, rows)], own)
    pl.semaphore_wait(barrier, count + 1)

    send_all(0, own, arrived)
    green_pair = rims(0, own, green_rims.at[0], green_rims.at[1])
    start_rims(green_pair)

    def keep_potential(k):
        row = first_row - 2 + k
        inside_row = jnp.clip(row, 0, rows_all - 1)
        for offset in range(5):
            column = row + offset - 2
            there = (row >= 0) & (row < rows_all) & (column >= 0) & (column < rows_all)
            flag = jnp.where(there, mask[inside_row, offset], 0)
            kept = (jnp.zeros((width, width), jnp.int32) + flag) > 0
            potential[k, :, offset * width:(offset + 1) * width] = jnp.where(
                kept, coulomb[inside_row, offset], jnp.zeros((), BF16))
    steps(row_count + 4, keep_potential)

    everything(0, own, arrived).wait_recv()
    unpack(arrived, slabs)

    def correlate(tile):
        a, b, c, d = waves(forward, slabs[2 * tile], slabs[2 * tile + 1])
        for part, value in enumerate((a, b, c, d)):
            spectra[tile, part] = value
        product_re = (a - b) * (a + b) - (c - d) * (c + d)
        product_im = 2.0 * (a * c + b * d)
        both = unwave(back_cos, jnp.concatenate([product_re, product_im], axis=1)) * scale
        slabs[2 * tile] = both[:, :width].astype(BF16)
        slabs[2 * tile + 1] = both[:, width:].astype(BF16)
    steps(rows // 2, correlate)
    pack(slabs, polar_sent)

    send_all(1, polar_sent, polar_blocks.at[1])
    end_rims(green_pair, green_rims.at[0], green_rims.at[1], green_tiles, rows)
    everything(1, polar_sent, polar_blocks.at[1]).wait_recv()
    polar_pair = rims(1, polar_blocks.at[1], polar_blocks.at[0], polar_blocks.at[2])
    start_rims(polar_pair)
    unpack(polar_blocks.at[1], window.at[pl.ds(rows, rows)])
    end_rims(polar_pair, polar_blocks.at[0], polar_blocks.at[2], window, rows)

    def tile_of(store, row, offset):
        return store[6 * row + 2 * offset], store[6 * row + 2 * offset + 1]

    def screen(row):
        for extent in range(-2, 5):
            total = None
            for middle in range(-2, 3):
                second = extent - middle
                if not -2 <= second <= 2:
                    continue
                left = potential[2 + row, :, (middle + 2) * width:(middle + 3) * width]
                if second >= 0:
                    right = jnp.concatenate(tile_of(window, 2 + row + middle, second), axis=1)
                    term = dot(left, right)
                else:
                    right = jnp.concatenate(tile_of(window, 2 + row + extent, -second), axis=0)
                    term = dot(left, right, True)
                total = term if total is None else total + term
            lanes = pl.ds((extent + 2) * width, width)
            mixed[pl.ds(0, width), lanes] = total[:, :width].astype(BF16)
            mixed[pl.ds(width, width), lanes] = total[:, width:].astype(BF16)
        for column in range(3):
            left = mixed[:, column * width:(column + 5) * width]
            result = dot(left, potential[2 + row + column], True)
            slabs[6 * row + 2 * column] = result[:width].astype(BF16)
            slabs[6 * row + 2 * column + 1] = result[width:].astype(BF16)
    steps(row_count, screen)
    pack(slabs, screen_sent)

    send_all(2, screen_sent, screen_blocks)
    everything(2, screen_sent, screen_blocks).wait_recv()
    unpack(screen_blocks, slabs)
    energies = lax.broadcasted_iota(jnp.int32, (points, 2 * width), 0)

    def convolve(tile):
        a, b, c, d = [spectra[tile, part] for part in range(4)]
        a2, b2, c2, d2 = waves(forward, slabs[2 * tile], slabs[2 * tile + 1])
        even_re = (a * a2 - c * c2) + (b * b2 - d * d2)
        even_im = (a * c2 + c * a2) - (b * d2 + d * b2)
        odd_re = (a * b2 + c * d2) + (b * a2 + d * c2)
        odd_im = (c * b2 - a * d2) + (b * c2 - d * a2)
        both = unwave(back_cos, jnp.concatenate([even_re, even_im], axis=1))
        both = both + unwave(back_sin, jnp.concatenate([-odd_im, odd_re], axis=1))
        first = window_lo[first_row + tile // 3]
        active = (energies >= first) & (energies < first + points // 2)
        both = jnp.where(active, both * scale, 0.0)
        slabs[2 * tile] = both[:, :width].astype(BF16)
        slabs[2 * tile + 1] = both[:, width:].astype(BF16)
    steps(rows // 2, convolve)
    pack(slabs, sigma_sent)

    send_all(3, sigma_sent, sigma_blocks.at[1])
    everything(3, sigma_sent, sigma_blocks.at[1]).wait_recv()
    sigma_pair = rims(2, sigma_blocks.at[1], sigma_blocks.at[0], sigma_blocks.at[2])
    start_rims(sigma_pair)
    unpack(sigma_blocks.at[1], window.at[pl.ds(rows, rows)])
    end_rims(sigma_pair, sigma_blocks.at[0], sigma_blocks.at[2], window, rows)

    def banded(store, row, offset):
        if offset >= 0:
            return tile_of(store, row, offset), False
        return tile_of(store, row + offset, -offset), True

    def dyson(row):
        lefts = []
        for middle in range(-2, 3):
            tile, flipped = banded(green_tiles, 2 + row, middle)
            parts = [tile[0].T, tile[1].T] if flipped else [tile[0], tile[1]]
            lefts.append(jnp.concatenate(parts, axis=1))
        products = []
        for extent in range(-2, 5):
            total = None
            for middle in range(-2, 3):
                second = extent - middle
                if not -2 <= second <= 2:
                    continue
                tile, flipped = banded(window, 2 + row + middle, second)
                term = dot(lefts[middle + 2], tile_right(tile, flipped), flipped)
                total = term if total is None else total + term
            products.append(total.astype(BF16))
        for column in range(3):
            total = None
            for extent in range(column - 2, column + 3):
                tile, flipped = banded(green_tiles, 2 + row + extent, column - extent)
                term = dot(products[extent + 2], tile_right(tile, flipped), flipped)
                total = term if total is None else total + term
            base = tile_of(green_tiles, 2 + row, column)
            for part in range(2):
                change = coupling * total[:, part * width:(part + 1) * width]
                out[6 * row + 2 * column + part] = (base[part].astype(F32) + change).astype(BF16)
    steps(row_count, dyson)

    for phase, source, landed in (
        (0, own, arrived), (1, polar_sent, polar_blocks.at[1]),
        (2, screen_sent, screen_blocks), (3, sigma_sent, sigma_blocks.at[1])):
        everything(phase, source, landed).wait_send()
    for pair in (green_pair, polar_pair, sigma_pair):
        sent_rims(pair)


def on_device(greens, coulomb, band_mask, window_lo):
    row_count = greens.shape[1]
    width = greens.shape[-1]
    count = lax.axis_size("energy")
    rows = 6 * row_count
    forward, back_cos, back_sin = wave_tables(count)
    block = (count, rows // 4, 4, width)
    smem = pl.BlockSpec(memory_space=pltpu.SMEM)
    updated = pl.pallas_call(
        functools.partial(update_kernel, 1.0 / (5 * width)),
        out_shape=jax.ShapeDtypeStruct((rows, width, width), BF16),
        in_specs=[VMEM, VMEM, smem, smem, VMEM, VMEM, VMEM],
        out_specs=VMEM,
        scratch_shapes=[
            pltpu.VMEM(block, BF16), pltpu.VMEM(block, BF16), pltpu.VMEM((2, *block), BF16),
            pltpu.VMEM(block, BF16), pltpu.VMEM((3, *block), BF16),
            pltpu.VMEM(block, BF16), pltpu.VMEM(block, BF16),
            pltpu.VMEM(block, BF16), pltpu.VMEM((3, *block), BF16),
            pltpu.VMEM((rows, width, width), BF16),
            pltpu.VMEM((rows // 2, 4, count, width), F32),
            pltpu.VMEM((3 * rows, width, width), BF16),
            pltpu.VMEM((3 * rows, width, width), BF16),
            pltpu.VMEM((row_count + 4, width, 5 * width), BF16),
            pltpu.VMEM((2 * width, 7 * width), BF16),
            pltpu.SemaphoreType.DMA((4,)), pltpu.SemaphoreType.DMA((4,)),
            pltpu.SemaphoreType.DMA((3, 2)), pltpu.SemaphoreType.DMA((3, 2)),
        ],
        compiler_params=pltpu.CompilerParams(collective_id=0, has_side_effects=True),
    )(greens.reshape(rows, width, width), coulomb, band_mask, window_lo, forward, back_cos, back_sin)
    return updated.reshape(greens.shape)


def solution(mesh):
    return jax.shard_map(
        on_device,
        mesh=mesh,
        in_specs=(P("energy", "space", None, None, None, None), P(), P(), P()),
        out_specs=P("energy", "space", None, None, None, None),
        check_vma=False,
    )
```

```python
import functools
import math

import jax
import jax.numpy as jnp
import numpy as np
from jax import lax
from jax.experimental import pallas as pl
from jax.experimental.pallas import tpu as pltpu
from jax.sharding import PartitionSpec as P

MESH = pl.DeviceIdType.MESH
F32 = jnp.float32
BF16 = jnp.bfloat16
VMEM = pl.BlockSpec(memory_space=pltpu.VMEM)


def dot(left, right, flipped=False):
    return lax.dot_general(
        left, right, (((1,), (1 if flipped else 0,)), ((), ())), preferred_element_type=F32)


def halves(values):
    upper = values.astype(BF16)
    return upper, (values - upper.astype(F32)).astype(BF16)


def wave_tables(points):
    angle = 2.0 * math.pi * np.outer(np.arange(points) + 0.5, np.arange(points)) / (2 * points)
    cos, sin = np.cos(angle), np.sin(angle)
    forward = np.concatenate([cos, sin], axis=0)
    return halves_of(forward), halves_of(cos.T), halves_of(sin.T)


def halves_of(table):
    upper = table.astype(jnp.bfloat16)
    lower = (table - upper.astype(np.float64)).astype(jnp.bfloat16)
    return np.stack([upper, lower])


def waves(forward, re, im):
    points = re.shape[0]
    both = jnp.concatenate([re, im], axis=1)
    spectrum = dot(forward[0], both) + dot(forward[1], both)
    width = re.shape[1]
    return (spectrum[:points, :width], spectrum[points:, width:],
            spectrum[:points, width:], spectrum[points:, :width])


def unwave(table, values):
    upper, lower = halves(values)
    return dot(table[0], upper) + dot(table[0], lower) + dot(table[1], upper)


def tile_right(tile, flipped):
    re, im = tile[0], tile[1]
    if flipped:
        return jnp.concatenate(
            [jnp.concatenate([re, -im], axis=1), jnp.concatenate([im, re], axis=1)], axis=0)
    return jnp.concatenate(
        [jnp.concatenate([re, im], axis=1), jnp.concatenate([-im, re], axis=1)], axis=0)


def steps(count, body):
    lax.fori_loop(0, count, lambda k, carry: (body(k), carry)[1], 0)


def pack(tiles, blocks):
    def group(g):
        blocks[:, g] = jnp.transpose(tiles[pl.ds(4 * g, 4)], (1, 0, 2))
    steps(blocks.shape[1], group)


def unpack(blocks, tiles):
    def group(g):
        tiles[pl.ds(4 * g, 4)] = jnp.transpose(blocks[:, g], (1, 0, 2))
    steps(blocks.shape[1], group)


FAR_FIRST = (4, 3, 5, 2, 6, 1, 7, 0)


def update_kernel(
    coupling, greens_in, coulomb_in, mask, window_lo, forward_in, cos_in, sin_in, out,
    own, arrived, green_rims, polar_sent, polar_blocks, screen_sent, screen_blocks,
    sigma_sent, sigma_blocks, slabs, spectra, green_tiles, window, potential, mixed,
    greens, coulomb, forward, back_cos, back_sin, in_sem,
    send_sem, recv_sem, rim_send, rim_recv,
):
    count = lax.axis_size("energy")
    sections = lax.axis_size("space")
    me = lax.axis_index("energy")
    section = lax.axis_index("space")
    row_count, width = greens.shape[0] // 6, greens.shape[-1]
    rows_all = coulomb.shape[0]
    points = count
    first_row = section * row_count
    scale = 1.0 / (count * math.sqrt(count))
    my_x, my_z, my_y = me // 64, me // 8 % 8, me % 8
    has_before, has_after = section > 0, section < sections - 1
    some = pl.ds(0, count - 1)

    along_y = [(my_y + offset) % 8 for offset in FAR_FIRST]
    along_z = [(my_z + offset) % 8 * 8 for offset in FAR_FIRST]
    others = [
        across + deep + high
        for across in ((my_x + 1) % 2 * 64, my_x * 64) for deep in along_z for high in along_y
    ][:-1]

    def with_partners(act):
        for peer in others:
            act(peer)

    def send_all(phase, source, landed):
        with_partners(lambda peer: pltpu.make_async_remote_copy(
            source.at[peer], landed.at[me], send_sem.at[phase], recv_sem.at[phase],
            device_id={"energy": peer}, device_id_type=MESH).start())
        landed[pl.ds(me, 1)] = source[pl.ds(me, 1)]

    def everything(phase, source, landed):
        return pltpu.make_async_remote_copy(
            source.at[some], landed.at[some], send_sem.at[phase], recv_sem.at[phase],
            device_id={"energy": (me + 1) % count}, device_id_type=MESH)

    def rims(phase, block, before, after):
        to_following = pltpu.make_async_remote_copy(
            block, before, rim_send.at[phase, 0], rim_recv.at[phase, 0],
            device_id={"space": (section + 1) % sections}, device_id_type=MESH)
        to_preceding = pltpu.make_async_remote_copy(
            block, after, rim_send.at[phase, 1], rim_recv.at[phase, 1],
            device_id={"space": (section + sections - 1) % sections}, device_id_type=MESH)
        return to_following, to_preceding

    def start_rims(pair):
        @pl.when(has_after)
        def _():
            pair[0].start()

        @pl.when(has_before)
        def _():
            pair[1].start()

    def end_rims(pair, before, after, tiles, rows):
        @pl.when(has_before)
        def _():
            pair[0].wait_recv()
            unpack(before, tiles.at[pl.ds(0, rows)])

        @pl.when(section == 0)
        def _():
            tiles[pl.ds(0, rows)] = jnp.zeros((rows, width, width), BF16)

        @pl.when(has_after)
        def _():
            pair[1].wait_recv()
            unpack(after, tiles.at[pl.ds(2 * rows, rows)])

        @pl.when(section == sections - 1)
        def _():
            tiles[pl.ds(2 * rows, rows)] = jnp.zeros((rows, width, width), BF16)

    def sent_rims(pair):
        @pl.when(has_after)
        def _():
            pair[0].wait_send()

        @pl.when(has_before)
        def _():
            pair[1].wait_send()

    barrier = pltpu.get_barrier_semaphore()
    with_partners(lambda peer: pl.semaphore_signal(
        barrier, inc=1, device_id={"energy": peer}, device_id_type=MESH))
    for step in (1, sections - 1):
        pl.semaphore_signal(
            barrier, inc=1, device_id={"space": (section + step) % sections}, device_id_type=MESH)

    loads = [
        pltpu.make_async_copy(source, target, in_sem.at[k])
        for k, (source, target) in enumerate((
            (greens_in, greens), (coulomb_in, coulomb), (forward_in, forward),
            (cos_in, back_cos), (sin_in, back_sin)))]
    for load in loads:
        load.start()

    rows = 6 * row_count
    loads[0].wait()

    def keep(k):
        row, offset = k // 6, k % 6 // 2
        kept = (jnp.zeros((width, width), jnp.int32) + (first_row + row + offset)) < rows_all
        green_tiles[rows + k] = jnp.where(kept, greens[k], jnp.zeros((), BF16))
    steps(rows, keep)
    pack(green_tiles.at[pl.ds(rows, rows)], own)
    loads[1].wait()

    def keep_potential(k):
        row = first_row - 2 + k
        inside_row = jnp.clip(row, 0, rows_all - 1)
        for offset in range(5):
            column = row + offset - 2
            there = (row >= 0) & (row < rows_all) & (column >= 0) & (column < rows_all)
            flag = jnp.where(there, mask[inside_row, offset], 0)
            kept = (jnp.zeros((width, width), jnp.int32) + flag) > 0
            potential[k, :, offset * width:(offset + 1) * width] = jnp.where(
                kept, coulomb[inside_row, offset], jnp.zeros((), BF16))
    steps(row_count + 4, keep_potential)
    for load in loads[2:]:
        load.wait()
    pl.semaphore_wait(barrier, count + 1)

    send_all(0, own, arrived)
    green_pair = rims(0, own, green_rims.at[0], green_rims.at[1])
    start_rims(green_pair)

    everything(0, own, arrived).wait_recv()
    unpack(arrived, slabs)

    def correlate(tile):
        a, b, c, d = waves(forward, slabs[2 * tile], slabs[2 * tile + 1])
        for part, value in enumerate((a, b, c, d)):
            spectra[tile, part] = value
        product_re = (a - b) * (a + b) - (c - d) * (c + d)
        product_im = 2.0 * (a * c + b * d)
        both = unwave(back_cos, jnp.concatenate([product_re, product_im], axis=1)) * scale
        slabs[2 * tile] = both[:, :width].astype(BF16)
        slabs[2 * tile + 1] = both[:, width:].astype(BF16)
    steps(rows // 2, correlate)
    pack(slabs, polar_sent)

    send_all(1, polar_sent, polar_blocks.at[1])
    end_rims(green_pair, green_rims.at[0], green_rims.at[1], green_tiles, rows)
    everything(1, polar_sent, polar_blocks.at[1]).wait_recv()
    polar_pair = rims(1, polar_blocks.at[1], polar_blocks.at[0], polar_blocks.at[2])
    start_rims(polar_pair)
    unpack(polar_blocks.at[1], window.at[pl.ds(rows, rows)])
    end_rims(polar_pair, polar_blocks.at[0], polar_blocks.at[2], window, rows)

    def tile_of(store, row, offset):
        return store[6 * row + 2 * offset], store[6 * row + 2 * offset + 1]

    def screen(row):
        for extent in range(-2, 5):
            total = None
            for middle in range(-2, 3):
                second = extent - middle
                if not -2 <= second <= 2:
                    continue
                left = potential[2 + row, :, (middle + 2) * width:(middle + 3) * width]
                if second >= 0:
                    right = jnp.concatenate(tile_of(window, 2 + row + middle, second), axis=1)
                    term = dot(left, right)
                else:
                    right = jnp.concatenate(tile_of(window, 2 + row + extent, -second), axis=0)
                    term = dot(left, right, True)
                total = term if total is None else total + term
            lanes = pl.ds((extent + 2) * width, width)
            mixed[pl.ds(0, width), lanes] = total[:, :width].astype(BF16)
            mixed[pl.ds(width, width), lanes] = total[:, width:].astype(BF16)
        for column in range(3):
            left = mixed[:, column * width:(column + 5) * width]
            result = dot(left, potential[2 + row + column], True)
            slabs[6 * row + 2 * column] = result[:width].astype(BF16)
            slabs[6 * row + 2 * column + 1] = result[width:].astype(BF16)
    steps(row_count, screen)
    pack(slabs, screen_sent)

    send_all(2, screen_sent, screen_blocks)
    everything(2, screen_sent, screen_blocks).wait_recv()
    unpack(screen_blocks, slabs)
    energies = lax.broadcasted_iota(jnp.int32, (points, 2 * width), 0)

    def convolve(tile):
        a, b, c, d = [spectra[tile, part] for part in range(4)]
        a2, b2, c2, d2 = waves(forward, slabs[2 * tile], slabs[2 * tile + 1])
        even_re = (a * a2 - c * c2) + (b * b2 - d * d2)
        even_im = (a * c2 + c * a2) - (b * d2 + d * b2)
        odd_re = (a * b2 + c * d2) + (b * a2 + d * c2)
        odd_im = (c * b2 - a * d2) + (b * c2 - d * a2)
        both = unwave(back_cos, jnp.concatenate([even_re, even_im], axis=1))
        both = both + unwave(back_sin, jnp.concatenate([-odd_im, odd_re], axis=1))
        first = window_lo[first_row + tile // 3]
        active = (energies >= first) & (energies < first + points // 2)
        both = jnp.where(active, both * scale, 0.0)
        slabs[2 * tile] = both[:, :width].astype(BF16)
        slabs[2 * tile + 1] = both[:, width:].astype(BF16)
    steps(rows // 2, convolve)
    pack(slabs, sigma_sent)

    send_all(3, sigma_sent, sigma_blocks.at[1])
    everything(3, sigma_sent, sigma_blocks.at[1]).wait_recv()
    sigma_pair = rims(2, sigma_blocks.at[1], sigma_blocks.at[0], sigma_blocks.at[2])
    start_rims(sigma_pair)
    unpack(sigma_blocks.at[1], window.at[pl.ds(rows, rows)])
    end_rims(sigma_pair, sigma_blocks.at[0], sigma_blocks.at[2], window, rows)

    def banded(store, row, offset):
        if offset >= 0:
            return tile_of(store, row, offset), False
        return tile_of(store, row + offset, -offset), True

    def dyson(row):
        lefts = []
        for middle in range(-2, 3):
            tile, flipped = banded(green_tiles, 2 + row, middle)
            parts = [tile[0].T, tile[1].T] if flipped else [tile[0], tile[1]]
            lefts.append(jnp.concatenate(parts, axis=1))
        products = []
        for extent in range(-2, 5):
            total = None
            for middle in range(-2, 3):
                second = extent - middle
                if not -2 <= second <= 2:
                    continue
                tile, flipped = banded(window, 2 + row + middle, second)
                term = dot(lefts[middle + 2], tile_right(tile, flipped), flipped)
                total = term if total is None else total + term
            products.append(total.astype(BF16))
        for column in range(3):
            total = None
            for extent in range(column - 2, column + 3):
                tile, flipped = banded(green_tiles, 2 + row + extent, column - extent)
                term = dot(products[extent + 2], tile_right(tile, flipped), flipped)
                total = term if total is None else total + term
            base = tile_of(green_tiles, 2 + row, column)
            for part in range(2):
                change = coupling * total[:, part * width:(part + 1) * width]
                out[6 * row + 2 * column + part] = (base[part].astype(F32) + change).astype(BF16)
    steps(row_count, dyson)

    for phase, source, landed in (
        (0, own, arrived), (1, polar_sent, polar_blocks.at[1]),
        (2, screen_sent, screen_blocks), (3, sigma_sent, sigma_blocks.at[1])):
        everything(phase, source, landed).wait_send()
    for pair in (green_pair, polar_pair, sigma_pair):
        sent_rims(pair)


def on_device(greens, coulomb, band_mask, window_lo):
    row_count = greens.shape[1]
    width = greens.shape[-1]
    count = lax.axis_size("energy")
    rows = 6 * row_count
    forward, back_cos, back_sin = wave_tables(count)
    block = (count, rows // 4, 4, width)
    smem = pl.BlockSpec(memory_space=pltpu.SMEM)
    away = pl.BlockSpec(memory_space=pl.ANY)
    updated = pl.pallas_call(
        functools.partial(update_kernel, 1.0 / (5 * width)),
        out_shape=jax.ShapeDtypeStruct((rows, width, width), BF16),
        in_specs=[away, away, smem, smem, away, away, away],
        out_specs=VMEM,
        scratch_shapes=[
            pltpu.VMEM(block, BF16), pltpu.VMEM(block, BF16), pltpu.VMEM((2, *block), BF16),
            pltpu.VMEM(block, BF16), pltpu.VMEM((3, *block), BF16),
            pltpu.VMEM(block, BF16), pltpu.VMEM(block, BF16),
            pltpu.VMEM(block, BF16), pltpu.VMEM((3, *block), BF16),
            pltpu.VMEM((rows, width, width), BF16),
            pltpu.VMEM((rows // 2, 4, count, width), F32),
            pltpu.VMEM((3 * rows, width, width), BF16),
            pltpu.VMEM((3 * rows, width, width), BF16),
            pltpu.VMEM((row_count + 4, width, 5 * width), BF16),
            pltpu.VMEM((2 * width, 7 * width), BF16),
            pltpu.VMEM((rows, width, width), BF16), pltpu.VMEM(coulomb.shape, BF16),
            pltpu.VMEM(forward.shape, BF16), pltpu.VMEM(back_cos.shape, BF16),
            pltpu.VMEM(back_sin.shape, BF16), pltpu.SemaphoreType.DMA((5,)),
            pltpu.SemaphoreType.DMA((4,)), pltpu.SemaphoreType.DMA((4,)),
            pltpu.SemaphoreType.DMA((3, 2)), pltpu.SemaphoreType.DMA((3, 2)),
        ],
        compiler_params=pltpu.CompilerParams(collective_id=0, has_side_effects=True),
    )(greens.reshape(rows, width, width), coulomb, band_mask, window_lo, forward, back_cos, back_sin)
    return updated.reshape(greens.shape)


def solution(mesh):
    return jax.shard_map(
        on_device,
        mesh=mesh,
        in_specs=(P("energy", "space", None, None, None, None), P(), P(), P()),
        out_specs=P("energy", "space", None, None, None, None),
        check_vma=False,
    )
```

```python
import functools
import math

import jax
import jax.numpy as jnp
import numpy as np
from jax import lax
from jax.experimental import pallas as pl
from jax.experimental.pallas import tpu as pltpu
from jax.sharding import PartitionSpec as P

MESH = pl.DeviceIdType.MESH
F32 = jnp.float32
BF16 = jnp.bfloat16
VMEM = pl.BlockSpec(memory_space=pltpu.VMEM)


def dot(left, right, flipped=False):
    return lax.dot_general(
        left, right, (((1,), (1 if flipped else 0,)), ((), ())), preferred_element_type=F32)


def halves(values):
    upper = values.astype(BF16)
    return upper, (values - upper.astype(F32)).astype(BF16)


def wave_tables(points):
    angle = 2.0 * math.pi * np.outer(np.arange(points) + 0.5, np.arange(points)) / (2 * points)
    cos, sin = np.cos(angle), np.sin(angle)
    forward = np.concatenate([cos, sin], axis=0)
    return halves_of(forward), halves_of(cos.T), halves_of(sin.T)


def halves_of(table):
    upper = table.astype(jnp.bfloat16)
    lower = (table - upper.astype(np.float64)).astype(jnp.bfloat16)
    return np.stack([upper, lower])


def waves(forward, re, im):
    points = re.shape[0]
    both = jnp.concatenate([re, im], axis=1)
    spectrum = dot(forward[0], both) + dot(forward[1], both)
    width = re.shape[1]
    return (spectrum[:points, :width], spectrum[points:, width:],
            spectrum[:points, width:], spectrum[points:, :width])


def unwave(table, values):
    upper, lower = halves(values)
    return dot(table[0], upper) + dot(table[0], lower) + dot(table[1], upper)


def tile_right(tile, flipped):
    re, im = tile[0], tile[1]
    if flipped:
        return jnp.concatenate(
            [jnp.concatenate([re, -im], axis=1), jnp.concatenate([im, re], axis=1)], axis=0)
    return jnp.concatenate(
        [jnp.concatenate([re, im], axis=1), jnp.concatenate([-im, re], axis=1)], axis=0)


def steps(count, body):
    lax.fori_loop(0, count, lambda k, carry: (body(k), carry)[1], 0)


def pack(tiles, blocks):
    def group(g):
        blocks[:, g] = jnp.transpose(tiles[pl.ds(4 * g, 4)], (1, 0, 2))
    steps(blocks.shape[1], group)


def unpack(blocks, tiles):
    def group(g):
        tiles[pl.ds(4 * g, 4)] = jnp.transpose(blocks[:, g], (1, 0, 2))
    steps(blocks.shape[1], group)


FAR_FIRST = (4, 3, 5, 2, 6, 1, 7, 0)


def update_kernel(
    coupling, greens_in, coulomb_in, mask, window_lo, forward_in, cos_in, sin_in, out,
    own, arrived, green_rims, polar_sent, polar_blocks, screen_sent, screen_blocks,
    sigma_sent, sigma_blocks, slabs, spectra, green_tiles, window, potential, mixed, sums,
    greens, coulomb, forward, back_cos, back_sin, in_sem,
    send_sem, recv_sem, rim_send, rim_recv,
):
    count = lax.axis_size("energy")
    sections = lax.axis_size("space")
    me = lax.axis_index("energy")
    section = lax.axis_index("space")
    row_count, width = greens.shape[0] // 6, greens.shape[-1]
    rows_all = coulomb.shape[0]
    points = count
    first_row = section * row_count
    scale = 1.0 / (count * math.sqrt(count))
    my_x, my_z, my_y = me // 64, me // 8 % 8, me % 8
    has_before, has_after = section > 0, section < sections - 1
    some = pl.ds(0, count - 1)

    along_y = [(my_y + offset) % 8 for offset in FAR_FIRST]
    along_z = [(my_z + offset) % 8 * 8 for offset in FAR_FIRST]
    others = [
        across + deep + high
        for across in ((my_x + 1) % 2 * 64, my_x * 64) for deep in along_z for high in along_y
    ][:-1]

    def with_partners(act):
        for peer in others:
            act(peer)

    def send_all(phase, source, landed):
        with_partners(lambda peer: pltpu.make_async_remote_copy(
            source.at[peer], landed.at[me], send_sem.at[phase], recv_sem.at[phase, my_x],
            device_id={"energy": peer}, device_id_type=MESH).start())
        landed[pl.ds(me, 1)] = source[pl.ds(me, 1)]

    def arrival(phase, source, landed, half):
        part = pl.ds(0, count // 2 - half)
        return pltpu.make_async_remote_copy(
            source.at[part], landed.at[part], send_sem.at[phase],
            recv_sem.at[phase, my_x if half else 1 - my_x],
            device_id={"energy": others[0]}, device_id_type=MESH)

    def wait_all(phase, source, landed):
        for half in range(2):
            arrival(phase, source, landed, half).wait_recv()

    def sent_all(phase, source, landed):
        pltpu.make_async_remote_copy(
            source.at[some], landed.at[some], send_sem.at[phase], recv_sem.at[phase, 0],
            device_id={"energy": others[0]}, device_id_type=MESH).wait_send()

    def rims(phase, block, before, after, half):
        part = pl.ds((my_x if half else 1 - my_x) * (count // 2), count // 2)
        to_following = pltpu.make_async_remote_copy(
            block.at[part], before.at[part], rim_send.at[phase, 0, half],
            rim_recv.at[phase, 0, half],
            device_id={"space": (section + 1) % sections}, device_id_type=MESH)
        to_preceding = pltpu.make_async_remote_copy(
            block.at[part], after.at[part], rim_send.at[phase, 1, half],
            rim_recv.at[phase, 1, half],
            device_id={"space": (section + sections - 1) % sections}, device_id_type=MESH)
        return to_following, to_preceding

    def start_rims(pair):
        @pl.when(has_after)
        def _():
            pair[0].start()

        @pl.when(has_before)
        def _():
            pair[1].start()

    def end_rims(pairs, before, after, tiles, rows):
        @pl.when(has_before)
        def _():
            for pair in pairs:
                pair[0].wait_recv()
            unpack(before, tiles.at[pl.ds(0, rows)])

        @pl.when(section == 0)
        def _():
            tiles[pl.ds(0, rows)] = jnp.zeros((rows, width, width), BF16)

        @pl.when(has_after)
        def _():
            for pair in pairs:
                pair[1].wait_recv()
            unpack(after, tiles.at[pl.ds(2 * rows, rows)])

        @pl.when(section == sections - 1)
        def _():
            tiles[pl.ds(2 * rows, rows)] = jnp.zeros((rows, width, width), BF16)

    def sent_rims(pairs):
        for pair in pairs:
            @pl.when(has_after)
            def _():
                pair[0].wait_send()

            @pl.when(has_before)
            def _():
                pair[1].wait_send()

    def wait_and_pass_on(phase, rim_phase, source, blocks):
        pairs = [rims(rim_phase, blocks.at[1], blocks.at[0], blocks.at[2], k) for k in range(2)]
        for half in range(2):
            arrival(phase, source, blocks.at[1], half).wait_recv()
            start_rims(pairs[half])
        return pairs

    barrier = pltpu.get_barrier_semaphore()
    with_partners(lambda peer: pl.semaphore_signal(
        barrier, inc=1, device_id={"energy": peer}, device_id_type=MESH))
    for step in (1, sections - 1):
        pl.semaphore_signal(
            barrier, inc=1, device_id={"space": (section + step) % sections}, device_id_type=MESH)

    loads = [
        pltpu.make_async_copy(source, target, in_sem.at[k])
        for k, (source, target) in enumerate((
            (greens_in, greens), (coulomb_in, coulomb), (forward_in, forward),
            (cos_in, back_cos), (sin_in, back_sin)))]
    for load in loads:
        load.start()

    rows = 6 * row_count
    loads[0].wait()

    def keep(k):
        row, offset = k // 6, k % 6 // 2
        kept = (jnp.zeros((width, width), jnp.int32) + (first_row + row + offset)) < rows_all
        green_tiles[rows + k] = jnp.where(kept, greens[k], jnp.zeros((), BF16))
    steps(rows, keep)
    pack(green_tiles.at[pl.ds(rows, rows)], own)
    loads[1].wait()

    def keep_potential(k):
        row = first_row - 2 + k
        inside_row = jnp.clip(row, 0, rows_all - 1)
        for offset in range(5):
            column = row + offset - 2
            there = (row >= 0) & (row < rows_all) & (column >= 0) & (column < rows_all)
            flag = jnp.where(there, mask[inside_row, offset], 0)
            kept = (jnp.zeros((width, width), jnp.int32) + flag) > 0
            potential[k, :, offset * width:(offset + 1) * width] = jnp.where(
                kept, coulomb[inside_row, offset], jnp.zeros((), BF16))
    steps(row_count + 4, keep_potential)
    for load in loads[2:]:
        load.wait()
    pl.semaphore_wait(barrier, count + 1)

    send_all(0, own, arrived)
    green_pairs = [rims(0, own, green_rims.at[0], green_rims.at[1], k) for k in range(2)]
    for pair in green_pairs:
        start_rims(pair)

    wait_all(0, own, arrived)
    unpack(arrived, slabs)

    def correlate(tile):
        a, b, c, d = waves(forward, slabs[2 * tile], slabs[2 * tile + 1])
        for part, value in enumerate((a, b, c, d)):
            spectra[tile, part] = value
        product_re = (a - b) * (a + b) - (c - d) * (c + d)
        product_im = 2.0 * (a * c + b * d)
        both = unwave(back_cos, jnp.concatenate([product_re, product_im], axis=1)) * scale
        slabs[2 * tile] = both[:, :width].astype(BF16)
        slabs[2 * tile + 1] = both[:, width:].astype(BF16)
    steps(rows // 2, correlate)
    pack(slabs, polar_sent)

    send_all(1, polar_sent, polar_blocks.at[1])
    end_rims(green_pairs, green_rims.at[0], green_rims.at[1], green_tiles, rows)
    polar_pairs = wait_and_pass_on(1, 1, polar_sent, polar_blocks)
    unpack(polar_blocks.at[1], window.at[pl.ds(rows, rows)])

    def tile_of(store, row, offset):
        return store[6 * row + 2 * offset], store[6 * row + 2 * offset + 1]

    def partial_sum(row, extent, term, own_rows):
        total = None
        for middle in range(-2, 3):
            stored = row + min(middle, extent)
            if abs(extent - middle) <= 2 and (0 <= stored < row_count) == own_rows:
                value = term(row, extent, middle)
                total = value if total is None else total + value
        return total

    def sum_own(term):
        for row in range(row_count):
            for extent in range(-2, 5):
                value = partial_sum(row, extent, term, True)
                if value is not None:
                    sums[row, extent + 2] = value

    def sum_rest(row, extent, term):
        value = partial_sum(row, extent, term, False)
        has_own = any(
            abs(extent - m) <= 2 and 0 <= row + min(m, extent) < row_count for m in range(-2, 3))
        if not has_own:
            return value
        held = sums[row, extent + 2]
        return held if value is None else held + value

    def screen_term(row, extent, middle):
        left = potential[2 + row, :, (middle + 2) * width:(middle + 3) * width]
        second = extent - middle
        if second >= 0:
            tile = tile_of(window, 2 + row + middle, second)
            return dot(left, jnp.concatenate(tile, axis=1))
        tile = tile_of(window, 2 + row + extent, -second)
        return dot(left, jnp.concatenate(tile, axis=0), True)

    sum_own(screen_term)
    end_rims(polar_pairs, polar_blocks.at[0], polar_blocks.at[2], window, rows)

    for row in range(row_count):
        for extent in range(-2, 5):
            total = sum_rest(row, extent, screen_term)
            lanes = pl.ds((extent + 2) * width, width)
            mixed[pl.ds(0, width), lanes] = total[:, :width].astype(BF16)
            mixed[pl.ds(width, width), lanes] = total[:, width:].astype(BF16)
        for column in range(3):
            left = mixed[:, column * width:(column + 5) * width]
            result = dot(left, potential[2 + row + column], True)
            slabs[6 * row + 2 * column] = result[:width].astype(BF16)
            slabs[6 * row + 2 * column + 1] = result[width:].astype(BF16)
    pack(slabs, screen_sent)

    send_all(2, screen_sent, screen_blocks)
    wait_all(2, screen_sent, screen_blocks)
    unpack(screen_blocks, slabs)
    energies = lax.broadcasted_iota(jnp.int32, (points, 2 * width), 0)

    def convolve(tile):
        a, b, c, d = [spectra[tile, part] for part in range(4)]
        a2, b2, c2, d2 = waves(forward, slabs[2 * tile], slabs[2 * tile + 1])
        even_re = (a * a2 - c * c2) + (b * b2 - d * d2)
        even_im = (a * c2 + c * a2) - (b * d2 + d * b2)
        odd_re = (a * b2 + c * d2) + (b * a2 + d * c2)
        odd_im = (c * b2 - a * d2) + (b * c2 - d * a2)
        both = unwave(back_cos, jnp.concatenate([even_re, even_im], axis=1))
        both = both + unwave(back_sin, jnp.concatenate([-odd_im, odd_re], axis=1))
        first = window_lo[first_row + tile // 3]
        active = (energies >= first) & (energies < first + points // 2)
        both = jnp.where(active, both * scale, 0.0)
        slabs[2 * tile] = both[:, :width].astype(BF16)
        slabs[2 * tile + 1] = both[:, width:].astype(BF16)
    steps(rows // 2, convolve)
    pack(slabs, sigma_sent)

    send_all(3, sigma_sent, sigma_blocks.at[1])
    sigma_pairs = wait_and_pass_on(3, 2, sigma_sent, sigma_blocks)
    unpack(sigma_blocks.at[1], window.at[pl.ds(rows, rows)])

    def banded(store, row, offset):
        if offset >= 0:
            return tile_of(store, row, offset), False
        return tile_of(store, row + offset, -offset), True

    lefts = []
    for row in range(row_count):
        for middle in range(-2, 3):
            tile, flipped = banded(green_tiles, 2 + row, middle)
            parts = [tile[0].T, tile[1].T] if flipped else [tile[0], tile[1]]
            lefts.append(jnp.concatenate(parts, axis=1))

    def dyson_term(row, extent, middle):
        tile, flipped = banded(window, 2 + row + middle, extent - middle)
        return dot(lefts[5 * row + middle + 2], tile_right(tile, flipped), flipped)

    sum_own(dyson_term)
    end_rims(sigma_pairs, sigma_blocks.at[0], sigma_blocks.at[2], window, rows)

    for row in range(row_count):
        products = [sum_rest(row, extent, dyson_term).astype(BF16) for extent in range(-2, 5)]
        for column in range(3):
            total = None
            for extent in range(column - 2, column + 3):
                tile, flipped = banded(green_tiles, 2 + row + extent, column - extent)
                term = dot(products[extent + 2], tile_right(tile, flipped), flipped)
                total = term if total is None else total + term
            base = tile_of(green_tiles, 2 + row, column)
            for part in range(2):
                change = coupling * total[:, part * width:(part + 1) * width]
                out[6 * row + 2 * column + part] = (base[part].astype(F32) + change).astype(BF16)

    for phase, source, landed in (
        (0, own, arrived), (1, polar_sent, polar_blocks.at[1]),
        (2, screen_sent, screen_blocks), (3, sigma_sent, sigma_blocks.at[1])):
        sent_all(phase, source, landed)
    for pairs in (green_pairs, polar_pairs, sigma_pairs):
        sent_rims(pairs)


def on_device(greens, coulomb, band_mask, window_lo):
    row_count = greens.shape[1]
    width = greens.shape[-1]
    count = lax.axis_size("energy")
    rows = 6 * row_count
    forward, back_cos, back_sin = wave_tables(count)
    block = (count, rows // 4, 4, width)
    smem = pl.BlockSpec(memory_space=pltpu.SMEM)
    away = pl.BlockSpec(memory_space=pl.ANY)
    updated = pl.pallas_call(
        functools.partial(update_kernel, 1.0 / (5 * width)),
        out_shape=jax.ShapeDtypeStruct((rows, width, width), BF16),
        in_specs=[away, away, smem, smem, away, away, away],
        out_specs=VMEM,
        scratch_shapes=[
            pltpu.VMEM(block, BF16), pltpu.VMEM(block, BF16), pltpu.VMEM((2, *block), BF16),
            pltpu.VMEM(block, BF16), pltpu.VMEM((3, *block), BF16),
            pltpu.VMEM(block, BF16), pltpu.VMEM(block, BF16),
            pltpu.VMEM(block, BF16), pltpu.VMEM((3, *block), BF16),
            pltpu.VMEM((rows, width, width), BF16),
            pltpu.VMEM((rows // 2, 4, count, width), F32),
            pltpu.VMEM((3 * rows, width, width), BF16),
            pltpu.VMEM((3 * rows, width, width), BF16),
            pltpu.VMEM((row_count + 4, width, 5 * width), BF16),
            pltpu.VMEM((2 * width, 7 * width), BF16),
            pltpu.VMEM((row_count, 7, width, 2 * width), F32),
            pltpu.VMEM((rows, width, width), BF16), pltpu.VMEM(coulomb.shape, BF16),
            pltpu.VMEM(forward.shape, BF16), pltpu.VMEM(back_cos.shape, BF16),
            pltpu.VMEM(back_sin.shape, BF16), pltpu.SemaphoreType.DMA((5,)),
            pltpu.SemaphoreType.DMA((4,)), pltpu.SemaphoreType.DMA((4, 2)),
            pltpu.SemaphoreType.DMA((3, 2, 2)), pltpu.SemaphoreType.DMA((3, 2, 2)),
        ],
        compiler_params=pltpu.CompilerParams(collective_id=0, has_side_effects=True),
    )(greens.reshape(rows, width, width), coulomb, band_mask, window_lo, forward, back_cos, back_sin)
    return updated.reshape(greens.shape)


def solution(mesh):
    return jax.shard_map(
        on_device,
        mesh=mesh,
        in_specs=(P("energy", "space", None, None, None, None), P(), P(), P()),
        out_specs=P("energy", "space", None, None, None, None),
        check_vma=False,
    )
```

```python
import functools
import math

import jax
import jax.numpy as jnp
import numpy as np
from jax import lax
from jax.experimental import pallas as pl
from jax.experimental.pallas import tpu as pltpu
from jax.sharding import PartitionSpec as P

MESH = pl.DeviceIdType.MESH
F32 = jnp.float32
BF16 = jnp.bfloat16
VMEM = pl.BlockSpec(memory_space=pltpu.VMEM)


def dot(left, right, flipped=False):
    return lax.dot_general(
        left, right, (((1,), (1 if flipped else 0,)), ((), ())), preferred_element_type=F32)


def halves(values):
    upper = values.astype(BF16)
    return upper, (values - upper.astype(F32)).astype(BF16)


def wave_tables(points):
    angle = 2.0 * math.pi * np.outer(np.arange(points) + 0.5, np.arange(points)) / (2 * points)
    cos, sin = np.cos(angle), np.sin(angle)
    forward = np.concatenate([cos, sin], axis=0)
    return halves_of(forward), halves_of(cos.T), halves_of(sin.T)


def halves_of(table):
    upper = table.astype(jnp.bfloat16)
    lower = (table - upper.astype(np.float64)).astype(jnp.bfloat16)
    return np.stack([upper, lower])


def waves(forward, re, im):
    points = re.shape[0]
    both = jnp.concatenate([re, im], axis=1)
    spectrum = dot(forward[0], both) + dot(forward[1], both)
    width = re.shape[1]
    return (spectrum[:points, :width], spectrum[points:, width:],
            spectrum[:points, width:], spectrum[points:, :width])


def unwave(table, values):
    upper, lower = halves(values)
    return dot(table[0], upper) + dot(table[0], lower) + dot(table[1], upper)


def tile_right(tile, flipped):
    re, im = tile[0], tile[1]
    if flipped:
        return jnp.concatenate(
            [jnp.concatenate([re, -im], axis=1), jnp.concatenate([im, re], axis=1)], axis=0)
    return jnp.concatenate(
        [jnp.concatenate([re, im], axis=1), jnp.concatenate([-im, re], axis=1)], axis=0)


def steps(count, body):
    lax.fori_loop(0, count, lambda k, carry: (body(k), carry)[1], 0)


def pack(tiles, blocks):
    def group(g):
        blocks[:, g] = jnp.transpose(tiles[pl.ds(4 * g, 4)], (1, 0, 2))
    steps(blocks.shape[1], group)


def unpack(blocks, tiles):
    def group(g):
        tiles[pl.ds(4 * g, 4)] = jnp.transpose(blocks[:, g], (1, 0, 2))
    steps(blocks.shape[1], group)


FAR_FIRST = (4, 3, 5, 2, 6, 1, 7, 0)


def update_kernel(
    coupling, greens_in, coulomb_in, mask, window_lo, forward_in, cos_in, sin_in, out,
    own, arrived, green_rims, polar_sent, polar_blocks, screen_sent, screen_blocks,
    sigma_sent, sigma_blocks, slabs, spectra, green_tiles, window, potential, mixed, sums,
    greens, coulomb, forward, back_cos, back_sin, in_sem,
    send_sem, recv_sem, rim_send, rim_recv,
):
    count = lax.axis_size("energy")
    sections = lax.axis_size("space")
    me = lax.axis_index("energy")
    section = lax.axis_index("space")
    row_count, width = greens.shape[0] // 6, greens.shape[-1]
    rows_all = coulomb.shape[0]
    points = count
    first_row = section * row_count
    scale = 1.0 / (count * math.sqrt(count))
    my_x, my_z, my_y = me // 64, me // 8 % 8, me % 8
    has_before, has_after = section > 0, section < sections - 1
    some = pl.ds(0, count - 1)

    along_y = [(my_y + offset) % 8 for offset in FAR_FIRST]
    along_z = [(my_z + offset) % 8 * 8 for offset in FAR_FIRST]
    others = [
        across + deep + high
        for across in ((my_x + 1) % 2 * 64, my_x * 64) for deep in along_z for high in along_y
    ][:-1]

    def with_partners(act):
        for peer in others:
            act(peer)

    def send_all(phase, source, landed):
        with_partners(lambda peer: pltpu.make_async_remote_copy(
            source.at[peer], landed.at[me], send_sem.at[phase], recv_sem.at[phase, my_x],
            device_id={"energy": peer}, device_id_type=MESH).start())
        landed[pl.ds(me, 1)] = source[pl.ds(me, 1)]

    def arrival(phase, source, landed, half):
        part = pl.ds(0, count // 2 - half)
        return pltpu.make_async_remote_copy(
            source.at[part], landed.at[part], send_sem.at[phase],
            recv_sem.at[phase, my_x if half else 1 - my_x],
            device_id={"energy": others[0]}, device_id_type=MESH)

    def wait_all(phase, source, landed):
        for half in range(2):
            arrival(phase, source, landed, half).wait_recv()

    def sent_all(phase, source, landed):
        pltpu.make_async_remote_copy(
            source.at[some], landed.at[some], send_sem.at[phase], recv_sem.at[phase, 0],
            device_id={"energy": others[0]}, device_id_type=MESH).wait_send()

    def rims(phase, block, before, after, half):
        part = pl.ds((my_x if half else 1 - my_x) * (count // 2), count // 2)
        to_following = pltpu.make_async_remote_copy(
            block.at[part], before.at[part], rim_send.at[phase, 0, half],
            rim_recv.at[phase, 0, half],
            device_id={"space": (section + 1) % sections}, device_id_type=MESH)
        to_preceding = pltpu.make_async_remote_copy(
            block.at[part], after.at[part], rim_send.at[phase, 1, half],
            rim_recv.at[phase, 1, half],
            device_id={"space": (section + sections - 1) % sections}, device_id_type=MESH)
        return to_following, to_preceding

    def start_rims(pair):
        @pl.when(has_after)
        def _():
            pair[0].start()

        @pl.when(has_before)
        def _():
            pair[1].start()

    def end_rims(pairs, before, after, tiles, rows):
        @pl.when(has_before)
        def _():
            for pair in pairs:
                pair[0].wait_recv()
            unpack(before, tiles.at[pl.ds(0, rows)])

        @pl.when(section == 0)
        def _():
            tiles[pl.ds(0, rows)] = jnp.zeros((rows, width, width), BF16)

        @pl.when(has_after)
        def _():
            for pair in pairs:
                pair[1].wait_recv()
            unpack(after, tiles.at[pl.ds(2 * rows, rows)])

        @pl.when(section == sections - 1)
        def _():
            tiles[pl.ds(2 * rows, rows)] = jnp.zeros((rows, width, width), BF16)

    def sent_rims(pairs):
        for pair in pairs:
            @pl.when(has_after)
            def _():
                pair[0].wait_send()

            @pl.when(has_before)
            def _():
                pair[1].wait_send()

    def wait_and_pass_on(phase, rim_phase, source, blocks):
        pairs = [rims(rim_phase, blocks.at[1], blocks.at[0], blocks.at[2], k) for k in range(2)]
        for half in range(2):
            arrival(phase, source, blocks.at[1], half).wait_recv()
            start_rims(pairs[half])
        return pairs

    barrier = pltpu.get_barrier_semaphore()
    with_partners(lambda peer: pl.semaphore_signal(
        barrier, inc=1, device_id={"energy": peer}, device_id_type=MESH))
    for step in (1, sections - 1):
        pl.semaphore_signal(
            barrier, inc=1, device_id={"space": (section + step) % sections}, device_id_type=MESH)

    loads = [
        pltpu.make_async_copy(source, target, in_sem.at[k])
        for k, (source, target) in enumerate((
            (greens_in, greens), (coulomb_in, coulomb), (forward_in, forward),
            (cos_in, back_cos), (sin_in, back_sin)))]
    for load in loads:
        load.start()

    rows = 6 * row_count
    loads[0].wait()

    def keep(k):
        row, offset = k // 6, k % 6 // 2
        kept = (jnp.zeros((width, width), jnp.int32) + (first_row + row + offset)) < rows_all
        green_tiles[rows + k] = jnp.where(kept, greens[k], jnp.zeros((), BF16))
    steps(rows, keep)
    pack(green_tiles.at[pl.ds(rows, rows)], own)
    loads[1].wait()

    def keep_potential(k):
        row = first_row - 2 + k
        inside_row = jnp.clip(row, 0, rows_all - 1)
        for offset in range(5):
            column = row + offset - 2
            there = (row >= 0) & (row < rows_all) & (column >= 0) & (column < rows_all)
            flag = jnp.where(there, mask[inside_row, offset], 0)
            kept = (jnp.zeros((width, width), jnp.int32) + flag) > 0
            potential[k, :, offset * width:(offset + 1) * width] = jnp.where(
                kept, coulomb[inside_row, offset], jnp.zeros((), BF16))
    steps(row_count + 4, keep_potential)
    for load in loads[2:]:
        load.wait()
    pl.semaphore_wait(barrier, count + 1)

    send_all(0, own, arrived)
    green_pairs = [rims(0, own, green_rims.at[0], green_rims.at[1], k) for k in range(2)]
    for pair in green_pairs:
        start_rims(pair)

    wait_all(0, own, arrived)
    unpack(arrived, slabs)

    def correlate(pair):
        tiles = (2 * pair, 2 * pair + 1)
        series = [(slabs[2 * tile], slabs[2 * tile + 1]) for tile in tiles]
        results = []
        for re, im in series:
            a, b, c, d = waves(forward, re, im)
            product_re = (a - b) * (a + b) - (c - d) * (c + d)
            product_im = 2.0 * (a * c + b * d)
            both = unwave(back_cos, jnp.concatenate([product_re, product_im], axis=1)) * scale
            results.append((both.astype(BF16), (a, b, c, d)))
        for tile, (both, values) in zip(tiles, results):
            for part, value in enumerate(values):
                spectra[tile, part] = value
            slabs[2 * tile] = both[:, :width]
            slabs[2 * tile + 1] = both[:, width:]
    steps(rows // 4, correlate)
    pack(slabs, polar_sent)

    send_all(1, polar_sent, polar_blocks.at[1])
    end_rims(green_pairs, green_rims.at[0], green_rims.at[1], green_tiles, rows)
    polar_pairs = wait_and_pass_on(1, 1, polar_sent, polar_blocks)
    unpack(polar_blocks.at[1], window.at[pl.ds(rows, rows)])

    def tile_of(store, row, offset):
        return store[6 * row + 2 * offset], store[6 * row + 2 * offset + 1]

    def partial_sum(row, extent, term, own_rows):
        total = None
        for middle in range(-2, 3):
            stored = row + min(middle, extent)
            if abs(extent - middle) <= 2 and (0 <= stored < row_count) == own_rows:
                value = term(row, extent, middle)
                total = value if total is None else total + value
        return total

    def sum_own(term):
        for row in range(row_count):
            for extent in range(-2, 5):
                value = partial_sum(row, extent, term, True)
                if value is not None:
                    sums[row, extent + 2] = value

    def sum_rest(row, extent, term):
        value = partial_sum(row, extent, term, False)
        has_own = any(
            abs(extent - m) <= 2 and 0 <= row + min(m, extent) < row_count for m in range(-2, 3))
        if not has_own:
            return value
        held = sums[row, extent + 2]
        return held if value is None else held + value

    def screen_term(row, extent, middle):
        left = potential[2 + row, :, (middle + 2) * width:(middle + 3) * width]
        second = extent - middle
        if second >= 0:
            tile = tile_of(window, 2 + row + middle, second)
            return dot(left, jnp.concatenate(tile, axis=1))
        tile = tile_of(window, 2 + row + extent, -second)
        return dot(left, jnp.concatenate(tile, axis=0), True)

    sum_own(screen_term)
    end_rims(polar_pairs, polar_blocks.at[0], polar_blocks.at[2], window, rows)

    for row in range(row_count):
        for extent in range(-2, 5):
            total = sum_rest(row, extent, screen_term)
            lanes = pl.ds((extent + 2) * width, width)
            mixed[pl.ds(0, width), lanes] = total[:, :width].astype(BF16)
            mixed[pl.ds(width, width), lanes] = total[:, width:].astype(BF16)
        for column in range(3):
            left = mixed[:, column * width:(column + 5) * width]
            result = dot(left, potential[2 + row + column], True)
            slabs[6 * row + 2 * column] = result[:width].astype(BF16)
            slabs[6 * row + 2 * column + 1] = result[width:].astype(BF16)
    pack(slabs, screen_sent)

    send_all(2, screen_sent, screen_blocks)
    wait_all(2, screen_sent, screen_blocks)
    unpack(screen_blocks, slabs)
    energies = lax.broadcasted_iota(jnp.int32, (points, 2 * width), 0)

    def convolve(pair):
        tiles = (2 * pair, 2 * pair + 1)
        series = [(slabs[2 * tile], slabs[2 * tile + 1]) for tile in tiles]
        results = []
        for tile, (re, im) in zip(tiles, series):
            a, b, c, d = [spectra[tile, part] for part in range(4)]
            a2, b2, c2, d2 = waves(forward, re, im)
            even_re = (a * a2 - c * c2) + (b * b2 - d * d2)
            even_im = (a * c2 + c * a2) - (b * d2 + d * b2)
            odd_re = (a * b2 + c * d2) + (b * a2 + d * c2)
            odd_im = (c * b2 - a * d2) + (b * c2 - d * a2)
            both = unwave(back_cos, jnp.concatenate([even_re, even_im], axis=1))
            both = both + unwave(back_sin, jnp.concatenate([-odd_im, odd_re], axis=1))
            first = window_lo[first_row + tile // 3]
            active = (energies >= first) & (energies < first + points // 2)
            results.append(jnp.where(active, both * scale, 0.0).astype(BF16))
        for tile, both in zip(tiles, results):
            slabs[2 * tile] = both[:, :width]
            slabs[2 * tile + 1] = both[:, width:]
    steps(rows // 4, convolve)
    pack(slabs, sigma_sent)

    send_all(3, sigma_sent, sigma_blocks.at[1])
    def banded(store, row, offset):
        if offset >= 0:
            return tile_of(store, row, offset), False
        return tile_of(store, row + offset, -offset), True

    lefts = []
    for row in range(row_count):
        for middle in range(-2, 3):
            tile, flipped = banded(green_tiles, 2 + row, middle)
            parts = [tile[0].T, tile[1].T] if flipped else [tile[0], tile[1]]
            lefts.append(jnp.concatenate(parts, axis=1))

    sigma_pairs = wait_and_pass_on(3, 2, sigma_sent, sigma_blocks)
    unpack(sigma_blocks.at[1], window.at[pl.ds(rows, rows)])

    def dyson_term(row, extent, middle):
        tile, flipped = banded(window, 2 + row + middle, extent - middle)
        return dot(lefts[5 * row + middle + 2], tile_right(tile, flipped), flipped)

    sum_own(dyson_term)
    end_rims(sigma_pairs, sigma_blocks.at[0], sigma_blocks.at[2], window, rows)

    for row in range(row_count):
        products = [sum_rest(row, extent, dyson_term).astype(BF16) for extent in range(-2, 5)]
        for column in range(3):
            total = None
            for extent in range(column - 2, column + 3):
                tile, flipped = banded(green_tiles, 2 + row + extent, column - extent)
                term = dot(products[extent + 2], tile_right(tile, flipped), flipped)
                total = term if total is None else total + term
            base = tile_of(green_tiles, 2 + row, column)
            for part in range(2):
                change = coupling * total[:, part * width:(part + 1) * width]
                out[6 * row + 2 * column + part] = (base[part].astype(F32) + change).astype(BF16)

    for phase, source, landed in (
        (0, own, arrived), (1, polar_sent, polar_blocks.at[1]),
        (2, screen_sent, screen_blocks), (3, sigma_sent, sigma_blocks.at[1])):
        sent_all(phase, source, landed)
    for pairs in (green_pairs, polar_pairs, sigma_pairs):
        sent_rims(pairs)


def on_device(greens, coulomb, band_mask, window_lo):
    row_count = greens.shape[1]
    width = greens.shape[-1]
    count = lax.axis_size("energy")
    rows = 6 * row_count
    forward, back_cos, back_sin = wave_tables(count)
    block = (count, rows // 4, 4, width)
    smem = pl.BlockSpec(memory_space=pltpu.SMEM)
    away = pl.BlockSpec(memory_space=pl.ANY)
    updated = pl.pallas_call(
        functools.partial(update_kernel, 1.0 / (5 * width)),
        out_shape=jax.ShapeDtypeStruct((rows, width, width), BF16),
        in_specs=[away, away, smem, smem, away, away, away],
        out_specs=VMEM,
        scratch_shapes=[
            pltpu.VMEM(block, BF16), pltpu.VMEM(block, BF16), pltpu.VMEM((2, *block), BF16),
            pltpu.VMEM(block, BF16), pltpu.VMEM((3, *block), BF16),
            pltpu.VMEM(block, BF16), pltpu.VMEM(block, BF16),
            pltpu.VMEM(block, BF16), pltpu.VMEM((3, *block), BF16),
            pltpu.VMEM((rows, width, width), BF16),
            pltpu.VMEM((rows // 2, 4, count, width), F32),
            pltpu.VMEM((3 * rows, width, width), BF16),
            pltpu.VMEM((3 * rows, width, width), BF16),
            pltpu.VMEM((row_count + 4, width, 5 * width), BF16),
            pltpu.VMEM((2 * width, 7 * width), BF16),
            pltpu.VMEM((row_count, 7, width, 2 * width), F32),
            pltpu.VMEM((rows, width, width), BF16), pltpu.VMEM(coulomb.shape, BF16),
            pltpu.VMEM(forward.shape, BF16), pltpu.VMEM(back_cos.shape, BF16),
            pltpu.VMEM(back_sin.shape, BF16), pltpu.SemaphoreType.DMA((5,)),
            pltpu.SemaphoreType.DMA((4,)), pltpu.SemaphoreType.DMA((4, 2)),
            pltpu.SemaphoreType.DMA((3, 2, 2)), pltpu.SemaphoreType.DMA((3, 2, 2)),
        ],
        compiler_params=pltpu.CompilerParams(collective_id=0, has_side_effects=True),
    )(greens.reshape(rows, width, width), coulomb, band_mask, window_lo, forward, back_cos, back_sin)
    return updated.reshape(greens.shape)


def solution(mesh):
    return jax.shard_map(
        on_device,
        mesh=mesh,
        in_specs=(P("energy", "space", None, None, None, None), P(), P(), P()),
        out_specs=P("energy", "space", None, None, None, None),
        check_vma=False,
    )
```
